128 devices in a mesh: section: 4 (over x_lo, core), seq: 8 (over x_hi, z), dp: 4 (over y).
Axes of the slice: x: 4 (x_hi: 2, x_lo: 2; x = x_hi * 2 + x_lo), y: 4, z: 4, core: 2. Of those that a mesh axis runs over, the one named last changes fastest.
Arguments:
- layer_input: bfloat16 [4, 8192, 16384], P('section', ('seq', 'dp')), may hold values from -6 to 6
- conv_weight: float32 [4, 4, 16384], P('section'), may hold values from -3 to 3
- conv_bias: float32 [4, 16384], P('section'), may hold values from -3 to 3
- log_decay: float32 [4, 8192, 256], P('section', ('seq', 'dp')), may hold values from -2 to 0, as said below
- state_write: bfloat16 [4, 16, 8192], P('section', None, ('seq', 'dp')), may hold values from -4 to 4
- state_read: bfloat16 [4, 16, 8192], P('section', None, ('seq', 'dp')), may hold values from -1.5 to 1.5
- skip_gain: float32 [4, 256], P('section'), may hold values from 0.5 to 2
- grad_out: bfloat16 [4, 8192, 16384], P('section', ('seq', 'dp')), may hold values from -6 to 6
Outputs:
- grad_prev: bfloat16 [4, 8192, 16384], P('section', ('seq', 'dp'))
- conv_weight_grad: float32 [4, 4, 16384], P('section', None, ('seq', 'dp'))
- conv_bias_grad: float32 [4, 16384], P('section', ('seq', 'dp'))
- skip_grad: float32 [4, 256], P('section', ('seq', 'dp'))
The draws below stay inside these ranges and needn't reach their ends.
Inputs may be any that keep to these rules, and one draw needn't show every extreme that they name: `log_decay`: negative.
All inputs are finite; a program needn't handle non-finite values.
Results may differ from the reference program's by a relative error of at most 0.0047.
Values may be sent and summed in bfloat16 or wider, within the bound.
A program may use at most 320 MiB of HBM per device.

```python
import jax
import jax.numpy as jnp
from jax import lax

INNER = 16384
STATE = 16
CONV = 4
STRETCH = 256
TOKENS_PER_SHARD = 256
DECAY_GROUP_HEADS = 256
MIXER_LAYER_COUNT = 4
SEQUENCE_TOKENS = 8192


def draw_log_decay(key, part):
    random_key_list = jax.random.split(key, 9)
    device_shard_count = SEQUENCE_TOKENS // TOKENS_PER_SHARD
    fast_share = 0.05
    middle_share = 0.45
    head_pick = jax.random.uniform(random_key_list[0], (MIXER_LAYER_COUNT, 1, 1, DECAY_GROUP_HEADS), jnp.float32, 0.0, 1.0)
    is_fast = head_pick < fast_share
    is_slow = head_pick >= fast_share + middle_share
    fast_rate = 1.0 / jax.random.uniform(random_key_list[1], (MIXER_LAYER_COUNT, 1, 1, DECAY_GROUP_HEADS), jnp.float32, 30.0, 50.0)
    middle_rate = jax.random.uniform(random_key_list[2], (MIXER_LAYER_COUNT, 1, 1, DECAY_GROUP_HEADS), jnp.float32, 1.2, 1.4) / TOKENS_PER_SHARD
    slow_head_count = jax.random.uniform(random_key_list[3], (MIXER_LAYER_COUNT, 1, 1, DECAY_GROUP_HEADS), jnp.float32, 0.6, 1.4) / device_shard_count
    device_factor = jnp.exp(jax.random.uniform(random_key_list[4], (MIXER_LAYER_COUNT, device_shard_count, 1, DECAY_GROUP_HEADS), jnp.float32, -0.35, 0.35))
    spike_strength = jax.random.uniform(random_key_list[5], (MIXER_LAYER_COUNT, device_shard_count, TOKENS_PER_SHARD, DECAY_GROUP_HEADS), jnp.float32, 0.5, 1.5)
    spike_token_index = jax.random.randint(random_key_list[6], (MIXER_LAYER_COUNT, device_shard_count, 1, DECAY_GROUP_HEADS), 0, TOKENS_PER_SHARD)
    token_shard_position = jnp.arange(TOKENS_PER_SHARD, dtype=jnp.int32)[None, None, :, None]
    spike_landed = (token_shard_position == spike_token_index).astype(jnp.float32)
    slow_decay_rates = slow_head_count * (0.2 * spike_strength / TOKENS_PER_SHARD + 0.8 * spike_landed)
    spread_rates = jnp.where(is_fast, fast_rate, middle_rate) * spike_strength
    shard_rates = jnp.where(is_slow, slow_decay_rates, spread_rates) * device_factor
    gentle_decay_rates = -shard_rates.reshape(MIXER_LAYER_COUNT, SEQUENCE_TOKENS, DECAY_GROUP_HEADS)
    spike_position = jax.random.randint(random_key_list[7], (MIXER_LAYER_COUNT, 2, 1), 0, SEQUENCE_TOKENS)
    token_position = jnp.arange(SEQUENCE_TOKENS, dtype=jnp.int32)[None, None, :]
    spike_struck = jnp.sum((token_position == spike_position).astype(jnp.float32), axis=1)
    spike_penalty = jnp.log(jax.random.uniform(random_key_list[8], (MIXER_LAYER_COUNT, 1, DECAY_GROUP_HEADS), jnp.float32, 0.5, 0.8))
    return (gentle_decay_rates + spike_struck[:, :, None] * spike_penalty).astype(jnp.float32)


def spiked(result, own_key, source, target, shards_of, factor):
    owner, partner = [(jnp.arange(result.shape[axis_at]) // (result.shape[axis_at] // shards_of)).reshape([-1 if axis == axis_at else 1 for axis in range(result.ndim)]) for axis_at in (source, target)]
    chosen = jax.random.permutation(own_key, shards_of)[partner]
    strong = (owner == chosen) | (owner == (partner + shards_of // 2) % shards_of)
    return jnp.where(strong, factor * result, result)


def block_scale(stream_key, shape, shards, smallest, top_value):
    def one(axis_at, shards_of):
        steps = jax.random.uniform(jax.random.fold_in(jax.random.fold_in(stream_key, 6), axis_at), (shards_of,), jnp.float32, smallest / len(shards), top_value / len(shards))
        return jnp.repeat(jnp.exp(steps), shape[axis_at] // shards_of).reshape((-1,) + (1,) * (len(shape) - axis_at - 1))

    level = one(*shards[0])
    for cut in shards[1:]:
        level = level * one(*cut)
    return level


def bell_draw(rng, dims, scale, most, shards=(), kind=jnp.bfloat16):
    result = scale * jax.random.normal(rng, dims, jnp.float32)
    if shards:
        result = result * block_scale(rng, dims, shards, -0.22, 0.18)
    return jnp.clip(result, -most, most).astype(kind)


def gaussian_with(stream_key, shape, scale, bound, cuts, heavy, held_as=jnp.bfloat16):
    values = scale * jax.random.normal(stream_key, shape, jnp.float32)
    if cuts:
        values = values * block_scale(stream_key, shape, cuts, -0.22, 0.18)
    return jnp.clip(spiked(values, jax.random.fold_in(stream_key, 3), *heavy), -bound, bound).astype(held_as)


def setup_inputs(seed: int = 0) -> dict:
    keys = jax.random.split(jax.random.key(seed), 9)
    layer_input = bell_draw(keys[0], (MIXER_LAYER_COUNT, SEQUENCE_TOKENS, INNER), 1.0, 6.0, ((0, 4), (1, 32)))
    conv_weight = bell_draw(keys[1], (MIXER_LAYER_COUNT, CONV, INNER), 0.5, 3.0, ((0, 4),), jnp.float32)
    conv_bias = bell_draw(keys[2], (MIXER_LAYER_COUNT, INNER), 0.5, 3.0, ((0, 4),), jnp.float32)
    log_decay = draw_log_decay(jax.random.fold_in(keys[8], 71), 0)
    state_write = bell_draw(keys[4], (MIXER_LAYER_COUNT, STATE, SEQUENCE_TOKENS), 0.25, 4.0, ((0, 4), (2, 32)))
    state_read = bell_draw(keys[5], (MIXER_LAYER_COUNT, STATE, SEQUENCE_TOKENS), 0.1, 1.5, ((0, 4), (2, 32)))
    skip_gain = jnp.clip(0.5 + 1.5 * jax.random.uniform(keys[6], (MIXER_LAYER_COUNT, DECAY_GROUP_HEADS), jnp.float32) ** block_scale(keys[6], (MIXER_LAYER_COUNT, DECAY_GROUP_HEADS), ((0, 4),), -0.2, 0.2), 0.5, 2.0)
    grad_out = gaussian_with(keys[7], (MIXER_LAYER_COUNT, SEQUENCE_TOKENS, INNER), 1.0, 6.0, ((0, 4), (1, 32)), (1, 2, 32, 2.75))
    return dict(layer_input=layer_input, conv_weight=conv_weight, conv_bias=conv_bias, log_decay=log_decay, state_write=state_write, state_read=state_read, skip_gain=skip_gain, grad_out=grad_out)


HIGH = lax.Precision.HIGHEST
group_heads = 32


def silu_slope(pre_act):
    sigma = jax.nn.sigmoid(pre_act)
    return sigma * (1.0 + pre_act * (1.0 - sigma))


def block_product(writes, readers, cumulative, upstream):
    scores = jnp.dot(writes.T, readers, preferred_element_type=jnp.float32)
    span_len = scores.shape[0]
    row_ids = lax.broadcasted_iota(jnp.int32, (span_len, span_len), 0)
    col_ids = lax.broadcasted_iota(jnp.int32, (span_len, span_len), 1)
    causal = col_ids >= row_ids
    head_count = cumulative.shape[1]
    group_size = min(group_heads, head_count)
    pieces = []
    for first_head in range(0, head_count, group_size):
        head_rates = cumulative[:, first_head:first_head + group_size].T
        spread = head_rates[:, None, :] - head_rates[:, :, None]
        weights = jnp.where(causal[None], jnp.exp(jnp.minimum(spread, 0.0)) * scores[None], 0.0).astype(jnp.bfloat16)
        pieces.append(jnp.einsum('hst,thp->shp', weights.astype(jnp.float32),
                                 upstream[:, first_head:first_head + group_size, :].astype(jnp.float32)))
    return jnp.concatenate(pieces, axis=1)


def block_summary(readers, cumulative, upstream):
    weighted = (readers.astype(jnp.float32)[None, :, :] * jnp.exp(cumulative).T[:, None, :]).astype(jnp.bfloat16)
    return jnp.einsum('hnt,thp->hnp', weighted.astype(jnp.float32), upstream.astype(jnp.float32))


def layer_backward(inputs, weight, bias_row, decay_rates, writes, readers, skip_row, upstream):
    token_count, channels = inputs.shape
    head_count = decay_rates.shape[1]
    head_size = channels // head_count
    state_size = writes.shape[0]
    tap_count = weight.shape[0]
    padded = jnp.concatenate([jnp.zeros((tap_count - 1, channels), jnp.bfloat16), inputs], axis=0)
    pre_act = jnp.broadcast_to(bias_row[None, :], (token_count, channels))
    for tap_pos in range(tap_count):
        begin = tap_count - 1 - tap_pos
        pre_act = pre_act + weight[tap_pos][None, :] * padded[begin:begin + token_count].astype(jnp.float32)
    active = jax.nn.silu(pre_act)
    blocks = token_count // STRETCH
    grad_heads = upstream.reshape(token_count, head_count, head_size)
    block_grads = grad_heads.reshape(blocks, STRETCH, head_count, head_size)
    block_rates = decay_rates.reshape(blocks, STRETCH, head_count)
    block_writes = writes.reshape(state_size, blocks, STRETCH).transpose(1, 0, 2)
    block_reads = readers.reshape(state_size, blocks, STRETCH).transpose(1, 0, 2)

    def one_block(carry_state, items):
        grad_blk, rate_blk, write_blk, read_blk = items
        cumulative = jnp.cumsum(rate_blk, axis=0)
        block_total = cumulative[-1]
        local_part = block_product(write_blk, read_blk, cumulative, grad_blk)
        carried_part = jnp.einsum('ns,hnp->shp', write_blk.astype(jnp.float32), carry_state, precision=HIGH)
        carried_part = carried_part * jnp.exp(block_total[None, :] - cumulative)[:, :, None]
        summary = block_summary(read_blk, cumulative, grad_blk)
        new_state = jnp.exp(block_total)[:, None, None] * carry_state + summary
        return new_state, local_part + carried_part

    start_state = jnp.zeros((head_count, state_size, head_size), jnp.float32)
    final_state, ssd_out = lax.scan(one_block, start_state, (block_grads, block_rates, block_writes, block_reads), reverse=True)
    ssd_out = ssd_out.reshape(token_count, head_count, head_size)
    grad_act = ssd_out + skip_row[None, :, None] * grad_heads.astype(jnp.float32)
    grad_act = grad_act.reshape(token_count, channels)
    skip_term = jnp.sum(grad_heads.astype(jnp.float32) * active.reshape(token_count, head_count, head_size), axis=(0, 2))
    grad_pre = grad_act * silu_slope(pre_act)
    extended = jnp.concatenate([grad_pre, jnp.zeros((tap_count - 1, channels), jnp.float32)], axis=0)
    input_grad = jnp.zeros((token_count, channels), jnp.float32)
    weight_terms = []
    for tap_pos in range(tap_count):
        input_grad = input_grad + weight[tap_pos][None, :] * extended[tap_pos:tap_pos + token_count]
        begin = tap_count - 1 - tap_pos
        weight_terms.append(jnp.sum(grad_pre * padded[begin:begin + token_count].astype(jnp.float32), axis=0))
    weight_grad = jnp.stack(weight_terms, axis=0)
    bias_grad = jnp.sum(grad_pre, axis=0)
    return input_grad.astype(jnp.bfloat16), weight_grad, bias_grad, skip_term


def reference(layer_input, conv_weight, conv_bias, log_decay, state_write, state_read, skip_gain, grad_out):
    def one_layer(items):
        return layer_backward(*items)

    input_grads, weight_grads, bias_grads, skip_grads = lax.map(
        one_layer, (layer_input, conv_weight, conv_bias, log_decay, state_write, state_read, skip_gain, grad_out))
    grad_prev = jnp.concatenate([input_grads[1:], jnp.zeros_like(input_grads[:1])], axis=0)
    return (grad_prev, weight_grads, bias_grads, skip_grads)
```

```python
import jax
import jax.numpy as jnp
from jax import lax
from jax.sharding import PartitionSpec as P

STRETCH = 256


HIGH = lax.Precision.HIGHEST
group_heads = 32


def from_behind(block, axis, distance):
    devices = range(lax.axis_size(axis))
    route = [(i - distance, i) for i in devices if i - distance in devices]
    return lax.ppermute(block, axis, route)


def shifted_from(part, axis, distance):
    count = lax.axis_size(axis)
    route = [(i + distance, i) for i in range(count) if i + distance < count]
    return jax.tree.map(lambda a: lax.ppermute(a, axis, route), part)


def carried_in(part, axis, combine):
    count = lax.axis_size(axis)
    state = shifted_from(part, axis, 1)
    distance = 1
    while distance < count - 1:
        state = combine(shifted_from(state, axis, distance), state)
        distance *= 2
    return state


def halving_scatter(rows, axis):
    count = lax.axis_size(axis)
    place = lax.axis_index(axis)
    mask = count // 2
    while mask >= 1:
        pairs = rows.reshape((2, rows.shape[0] // 2) + rows.shape[1:])
        upper = (place // mask) % 2 == 1
        keep = jnp.where(upper, pairs[1], pairs[0])
        send = jnp.where(upper, pairs[0], pairs[1])
        route = [(i, i ^ mask) for i in range(count)]
        rows = keep + lax.ppermute(send, axis, route)
        mask //= 2
    return rows[0]


def silu_slope(pre_act):
    sigma = jax.nn.sigmoid(pre_act)
    return sigma * (1.0 + pre_act * (1.0 - sigma))


def later_first(earlier, later):
    decay_high, state_high = earlier
    decay_low, state_low = later
    return (decay_low * decay_high, state_low + decay_low[:, None, None] * state_high)


def block_product(writes, readers, cumulative, upstream):
    scores = lax.dot_general(
        writes, readers, (((0,), (0,)), ((), ())), preferred_element_type=jnp.float32
    )
    span_len = scores.shape[0]
    row_ids = lax.broadcasted_iota(jnp.int32, (span_len, span_len), 0)
    col_ids = lax.broadcasted_iota(jnp.int32, (span_len, span_len), 1)
    causal = col_ids >= row_ids
    head_count = cumulative.shape[1]
    group_size = min(group_heads, head_count)
    pieces = []
    for first_head in range(0, head_count, group_size):
        head_rates = cumulative[:, first_head : first_head + group_size].T
        spread = head_rates[:, None, :] - head_rates[:, :, None]
        weights = jnp.where(
            causal[None], jnp.exp(jnp.minimum(spread, 0.0)) * scores[None], 0.0
        ).astype(jnp.bfloat16)
        pieces.append(
            jnp.einsum(
                "hst,thp->shp",
                weights,
                upstream[:, first_head : first_head + group_size, :],
                preferred_element_type=jnp.float32,
            )
        )
    return jnp.concatenate(pieces, axis=1)


def block_summary(readers, cumulative, upstream):
    weighted = (readers.astype(jnp.float32)[None, :, :] * jnp.exp(cumulative).T[:, None, :]).astype(
        jnp.bfloat16
    )
    return jnp.einsum("hnt,thp->hnp", weighted, upstream, preferred_element_type=jnp.float32)


def on_device(
    layer_input, conv_weight, conv_bias, log_decay, state_write, state_read, skip_gain, grad_out
):
    inputs = layer_input[0]
    weight = conv_weight[0]
    bias_row = conv_bias[0]
    decay_rates = log_decay[0]
    writes = state_write[0]
    readers = state_read[0]
    skip_row = skip_gain[0]
    upstream = grad_out[0]
    token_count, channels = inputs.shape
    head_count = decay_rates.shape[1]
    head_size = channels // head_count
    state_size = writes.shape[0]
    tap_count = weight.shape[0]
    prior_rows = from_behind(inputs[token_count - (tap_count - 1) :], ("seq", "dp"), 1)
    padded = jnp.concatenate([prior_rows, inputs], axis=0)
    pre_act = jnp.broadcast_to(bias_row[None, :], (token_count, channels))
    for tap_pos in range(tap_count):
        begin = tap_count - 1 - tap_pos
        pre_act = pre_act + weight[tap_pos][None, :] * padded[begin : begin + token_count].astype(
            jnp.float32
        )
    active = jax.nn.silu(pre_act)
    blocks = token_count // STRETCH
    grad_heads = upstream.reshape(token_count, head_count, head_size)
    block_idx = 0
    cumulative = jnp.cumsum(decay_rates, axis=0)
    local_parts = [block_product(writes, readers, cumulative, grad_heads)]
    summaries = [block_summary(readers, cumulative, grad_heads)]
    cumulatives = [cumulative]
    device_decay = jnp.ones((head_count,), jnp.float32)
    device_state = jnp.zeros((head_count, state_size, head_size), jnp.float32)
    for block_idx in reversed(range(blocks)):
        device_decay, device_state = later_first(
            (device_decay, device_state),
            (jnp.exp(cumulatives[block_idx][-1]), summaries[block_idx]),
        )
    carried = carried_in((device_decay, device_state), ("seq", "dp"), later_first)
    carry_state = carried[1]
    outputs = [None] * blocks
    for block_idx in reversed(range(blocks)):
        cumulative = cumulatives[block_idx]
        block_total = cumulative[-1]
        carried_part = jnp.einsum(
            "ns,hnp->shp", writes.astype(jnp.float32), carry_state, precision=HIGH
        )
        carried_part = carried_part * jnp.exp(block_total[None, :] - cumulative)[:, :, None]
        outputs[block_idx] = local_parts[block_idx] + carried_part
        carry_state = jnp.exp(block_total)[:, None, None] * carry_state + summaries[block_idx]
    ssd_out = outputs[0]
    grad_act = ssd_out + skip_row[None, :, None] * grad_heads.astype(jnp.float32)
    grad_act = grad_act.reshape(token_count, channels)
    skip_term = jnp.sum(
        grad_heads.astype(jnp.float32) * active.reshape(token_count, head_count, head_size),
        axis=(0, 2),
    )
    grad_pre = grad_act * silu_slope(pre_act)
    after_rows = from_behind(grad_pre[: tap_count - 1], ("seq", "dp"), -1)
    extended = jnp.concatenate([grad_pre, after_rows], axis=0)
    input_grad = jnp.zeros((token_count, channels), jnp.float32)
    weight_terms = []
    for tap_pos in range(tap_count):
        input_grad = (
            input_grad + weight[tap_pos][None, :] * extended[tap_pos : tap_pos + token_count]
        )
        begin = tap_count - 1 - tap_pos
        weight_terms.append(
            jnp.sum(grad_pre * padded[begin : begin + token_count].astype(jnp.float32), axis=0)
        )
    weight_grad = jnp.stack(weight_terms, axis=0)
    bias_grad = jnp.sum(grad_pre, axis=0)
    group = ("seq", "dp")
    parts = lax.axis_size(group)
    width = channels // parts
    packed = jnp.concatenate(
        [
            weight_grad.reshape(tap_count, parts, width).transpose(1, 0, 2).reshape(parts, tap_count * width),
            bias_grad.reshape(parts, width),
            skip_term.reshape(parts, head_count // parts),
        ],
        axis=1,
    )
    owned = halving_scatter(packed, group)
    shares = (
        owned[: tap_count * width].reshape(tap_count, width),
        owned[tap_count * width : (tap_count + 1) * width],
        owned[(tap_count + 1) * width :],
    )
    passed = from_behind(input_grad.astype(jnp.bfloat16)[None], "section", -1)
    return (passed, shares[0][None], shares[1][None], shares[2][None])


def solution(mesh):
    placed = (
        P("section", ("seq", "dp"), None),
        P("section", None, None),
        P("section", None),
        P("section", ("seq", "dp"), None),
        P("section", None, ("seq", "dp")),
        P("section", None, ("seq", "dp")),
        P("section", None),
        P("section", ("seq", "dp"), None),
    )
    return jax.shard_map(
        on_device,
        mesh=mesh,
        in_specs=placed,
        out_specs=(
            P("section", ("seq", "dp"), None),
            P("section", None, ("seq", "dp")),
            P("section", ("seq", "dp")),
            P("section", ("seq", "dp")),
        ),
        check_vma=False,
    )
```

```python
import jax
import jax.numpy as jnp
from jax import lax
from jax.sharding import PartitionSpec as P

STRETCH = 256


HIGH = lax.Precision.HIGHEST
group_heads = 32


def from_behind(block, axis, distance):
    devices = range(lax.axis_size(axis))
    route = [(i - distance, i) for i in devices if i - distance in devices]
    return lax.ppermute(block, axis, route)


def shifted_from(part, axis, distance):
    count = lax.axis_size(axis)
    route = [(i + distance, i) for i in range(count) if i + distance < count]
    return jax.tree.map(lambda a: lax.ppermute(a, axis, route), part)


def carried_in(part, axis, combine):
    count = lax.axis_size(axis)
    state = shifted_from(part, axis, 1)
    distance = 1
    while distance < count - 1:
        state = combine(shifted_from(state, axis, distance), state)
        distance *= 2
    return state


def halving_scatter(rows, axis):
    count = lax.axis_size(axis)
    place = lax.axis_index(axis)
    mask = count // 2
    while mask >= 1:
        pairs = rows.reshape((2, rows.shape[0] // 2) + rows.shape[1:])
        upper = (place // mask) % 2 == 1
        keep = jnp.where(upper, pairs[1], pairs[0])
        send = jnp.where(upper, pairs[0], pairs[1])
        route = [(i, i ^ mask) for i in range(count)]
        rows = keep + lax.ppermute(send, axis, route)
        mask //= 2
    return rows[0]


def silu_slope(pre_act):
    sigma = jax.nn.sigmoid(pre_act)
    return sigma * (1.0 + pre_act * (1.0 - sigma))


def later_first(earlier, later):
    decay_high, state_high = earlier
    decay_low, state_low = later
    return (decay_low * decay_high, state_low + decay_low[:, None, None] * state_high)


def block_product(writes, readers, cumulative, upstream):
    scores = lax.dot_general(
        writes, readers, (((0,), (0,)), ((), ())), preferred_element_type=jnp.float32
    )
    span_len = scores.shape[0]
    row_ids = lax.broadcasted_iota(jnp.int32, (span_len, span_len), 0)
    col_ids = lax.broadcasted_iota(jnp.int32, (span_len, span_len), 1)
    causal = col_ids >= row_ids
    head_count = cumulative.shape[1]
    group_size = min(group_heads, head_count)
    pieces = []
    for first_head in range(0, head_count, group_size):
        head_rates = cumulative[:, first_head : first_head + group_size].T
        spread = head_rates[:, None, :] - head_rates[:, :, None]
        weights = jnp.where(
            causal[None], jnp.exp(jnp.minimum(spread, 0.0)) * scores[None], 0.0
        ).astype(jnp.bfloat16)
        pieces.append(
            jnp.einsum(
                "hst,thp->shp",
                weights,
                upstream[:, first_head : first_head + group_size, :],
                preferred_element_type=jnp.float32,
            )
        )
    return jnp.concatenate(pieces, axis=1)


def block_summary(readers, cumulative, upstream):
    weighted = (readers.astype(jnp.float32)[None, :, :] * jnp.exp(cumulative).T[:, None, :]).astype(
        jnp.bfloat16
    )
    return jnp.einsum("hnt,thp->hnp", weighted, upstream, preferred_element_type=jnp.float32)


def conv_grads(grad_pre, padded, weight):
    token_count = grad_pre.shape[0]
    tap_count = weight.shape[0]
    after_rows = from_behind(grad_pre[: tap_count - 1], ("seq", "dp"), -1)
    extended = jnp.concatenate([grad_pre, after_rows], axis=0)
    input_grad = jnp.zeros(grad_pre.shape, jnp.float32)
    weight_terms = []
    for tap_pos in range(tap_count):
        input_grad = (
            input_grad + weight[tap_pos][None, :] * extended[tap_pos : tap_pos + token_count]
        )
        begin = tap_count - 1 - tap_pos
        weight_terms.append(
            jnp.sum(grad_pre * padded[begin : begin + token_count].astype(jnp.float32), axis=0)
        )
    return input_grad, jnp.stack(weight_terms, axis=0), jnp.sum(grad_pre, axis=0)


def on_device(
    layer_input, conv_weight, conv_bias, log_decay, state_write, state_read, skip_gain, grad_out
):
    inputs = layer_input[0]
    weight = conv_weight[0]
    bias_row = conv_bias[0]
    decay_rates = log_decay[0]
    writes = state_write[0]
    readers = state_read[0]
    skip_row = skip_gain[0]
    upstream = grad_out[0]
    token_count, channels = inputs.shape
    head_count = decay_rates.shape[1]
    head_size = channels // head_count
    state_size = writes.shape[0]
    tap_count = weight.shape[0]
    prior_rows = from_behind(inputs[token_count - (tap_count - 1) :], ("seq", "dp"), 1)
    padded = jnp.concatenate([prior_rows, inputs], axis=0)
    pre_act = jnp.broadcast_to(bias_row[None, :], (token_count, channels))
    for tap_pos in range(tap_count):
        begin = tap_count - 1 - tap_pos
        pre_act = pre_act + weight[tap_pos][None, :] * padded[begin : begin + token_count].astype(
            jnp.float32
        )
    active = jax.nn.silu(pre_act)
    blocks = token_count // STRETCH
    grad_heads = upstream.reshape(token_count, head_count, head_size)
    block_idx = 0
    cumulative = jnp.cumsum(decay_rates, axis=0)
    local_parts = [block_product(writes, readers, cumulative, grad_heads)]
    summaries = [block_summary(readers, cumulative, grad_heads)]
    cumulatives = [cumulative]
    device_decay = jnp.ones((head_count,), jnp.float32)
    device_state = jnp.zeros((head_count, state_size, head_size), jnp.float32)
    for block_idx in reversed(range(blocks)):
        device_decay, device_state = later_first(
            (device_decay, device_state),
            (jnp.exp(cumulatives[block_idx][-1]), summaries[block_idx]),
        )
    skip_term = jnp.sum(
        grad_heads.astype(jnp.float32) * active.reshape(token_count, head_count, head_size),
        axis=(0, 2),
    )
    slope = silu_slope(pre_act)
    cumulative = cumulatives[0]
    block_total = cumulative[-1]
    local_act = local_parts[0] + skip_row[None, :, None] * grad_heads.astype(jnp.float32)
    early = conv_grads(local_act.reshape(token_count, channels) * slope, padded, weight)
    early = lax.optimization_barrier((early, skip_term))
    carried = carried_in((device_decay, device_state), ("seq", "dp"), later_first)
    carry_state = carried[1]
    carried_part = jnp.einsum(
        "ns,hnp->shp", writes.astype(jnp.float32), carry_state, precision=HIGH
    )
    carried_part = carried_part * jnp.exp(block_total[None, :] - cumulative)[:, :, None]
    late = conv_grads(carried_part.reshape(token_count, channels) * slope, padded, weight)
    (early_input, early_weight, early_bias), skip_term = early
    input_grad = early_input + late[0]
    weight_grad = early_weight + late[1]
    bias_grad = early_bias + late[2]
    group = ("seq", "dp")
    parts = lax.axis_size(group)
    width = channels // parts
    packed = jnp.concatenate(
        [
            weight_grad.reshape(tap_count, parts, width).transpose(1, 0, 2).reshape(parts, tap_count * width),
            bias_grad.reshape(parts, width),
            skip_term.reshape(parts, head_count // parts),
        ],
        axis=1,
    )
    owned = halving_scatter(packed, group)
    shares = (
        owned[: tap_count * width].reshape(tap_count, width),
        owned[tap_count * width : (tap_count + 1) * width],
        owned[(tap_count + 1) * width :],
    )
    passed = from_behind(input_grad.astype(jnp.bfloat16)[None], "section", -1)
    return (passed, shares[0][None], shares[1][None], shares[2][None])


def solution(mesh):
    placed = (
        P("section", ("seq", "dp"), None),
        P("section", None, None),
        P("section", None),
        P("section", ("seq", "dp"), None),
        P("section", None, ("seq", "dp")),
        P("section", None, ("seq", "dp")),
        P("section", None),
        P("section", ("seq", "dp"), None),
    )
    return jax.shard_map(
        on_device,
        mesh=mesh,
        in_specs=placed,
        out_specs=(
            P("section", ("seq", "dp"), None),
            P("section", None, ("seq", "dp")),
            P("section", ("seq", "dp")),
            P("section", ("seq", "dp")),
        ),
        check_vma=False,
    )
```

```python
import jax
import jax.numpy as jnp
from jax import lax
from jax.sharding import PartitionSpec as P

STRETCH = 256


HIGH = lax.Precision.HIGHEST
group_heads = 32


def from_behind(block, axis, distance):
    devices = range(lax.axis_size(axis))
    route = [(i - distance, i) for i in devices if i - distance in devices]
    return lax.ppermute(block, axis, route)


def shifted_from(part, axis, distance):
    count = lax.axis_size(axis)
    route = [(i + distance, i) for i in range(count) if i + distance < count]
    return jax.tree.map(lambda a: lax.ppermute(a, axis, route), part)


def carried_in(part, axis, combine):
    count = lax.axis_size(axis)
    state = shifted_from(part, axis, 1)
    distance = 1
    while distance < count - 1:
        state = combine(shifted_from(state, axis, distance), state)
        distance *= 2
    return state


def halving_scatter(rows, axis):
    count = lax.axis_size(axis)
    place = lax.axis_index(axis)
    mask = count // 2
    while mask >= 1:
        pairs = rows.reshape((2, rows.shape[0] // 2) + rows.shape[1:])
        upper = (place // mask) % 2 == 1
        keep = jnp.where(upper, pairs[1], pairs[0])
        send = jnp.where(upper, pairs[0], pairs[1])
        route = [(i, i ^ mask) for i in range(count)]
        rows = keep + lax.ppermute(send, axis, route)
        mask //= 2
    return rows[0]


def silu_slope(pre_act):
    sigma = jax.nn.sigmoid(pre_act)
    return sigma * (1.0 + pre_act * (1.0 - sigma))


def later_first(earlier, later):
    decay_high, state_high = earlier
    decay_low, state_low = later
    return (decay_low * decay_high, state_low + decay_low[:, None, None] * state_high)


def block_product(writes, readers, cumulative, upstream):
    scores = lax.dot_general(
        writes, readers, (((0,), (0,)), ((), ())), preferred_element_type=jnp.float32
    )
    span_len = scores.shape[0]
    row_ids = lax.broadcasted_iota(jnp.int32, (span_len, span_len), 0)
    col_ids = lax.broadcasted_iota(jnp.int32, (span_len, span_len), 1)
    causal = col_ids >= row_ids
    head_count = cumulative.shape[1]
    group_size = min(group_heads, head_count)
    pieces = []
    for first_head in range(0, head_count, group_size):
        head_rates = cumulative[:, first_head : first_head + group_size].T
        spread = head_rates[:, None, :] - head_rates[:, :, None]
        weights = jnp.where(
            causal[None], jnp.exp(jnp.minimum(spread, 0.0)) * scores[None], 0.0
        ).astype(jnp.bfloat16)
        pieces.append(
            jnp.einsum(
                "hst,thp->shp",
                weights,
                upstream[:, first_head : first_head + group_size, :],
                preferred_element_type=jnp.float32,
            )
        )
    return jnp.concatenate(pieces, axis=1)


def block_summary(readers, cumulative, upstream):
    weighted = (readers.astype(jnp.float32)[None, :, :] * jnp.exp(cumulative).T[:, None, :]).astype(
        jnp.bfloat16
    )
    return jnp.einsum("hnt,thp->hnp", weighted, upstream, preferred_element_type=jnp.float32)


def conv_grads(grad_pre, padded, weight):
    token_count = grad_pre.shape[0]
    tap_count = weight.shape[0]
    after_rows = from_behind(grad_pre[: tap_count - 1], ("seq", "dp"), -1)
    extended = jnp.concatenate([grad_pre, after_rows], axis=0)
    input_grad = jnp.zeros(grad_pre.shape, jnp.float32)
    weight_terms = []
    for tap_pos in range(tap_count):
        input_grad = (
            input_grad + weight[tap_pos][None, :] * extended[tap_pos : tap_pos + token_count]
        )
        begin = tap_count - 1 - tap_pos
        weight_terms.append(
            jnp.sum(grad_pre * padded[begin : begin + token_count].astype(jnp.float32), axis=0)
        )
    return input_grad, jnp.stack(weight_terms, axis=0), jnp.sum(grad_pre, axis=0)


def on_device(
    layer_input, conv_weight, conv_bias, log_decay, state_write, state_read, skip_gain, grad_out
):
    inputs = layer_input[0]
    weight = conv_weight[0]
    bias_row = conv_bias[0]
    decay_rates = log_decay[0]
    writes = state_write[0]
    readers = state_read[0]
    skip_row = skip_gain[0]
    upstream = grad_out[0]
    token_count, channels = inputs.shape
    head_count = decay_rates.shape[1]
    head_size = channels // head_count
    state_size = writes.shape[0]
    tap_count = weight.shape[0]
    prior_rows = from_behind(inputs[token_count - (tap_count - 1) :], ("seq", "dp"), 1)
    padded = jnp.concatenate([prior_rows, inputs], axis=0)
    pre_act = jnp.broadcast_to(bias_row[None, :], (token_count, channels))
    for tap_pos in range(tap_count):
        begin = tap_count - 1 - tap_pos
        pre_act = pre_act + weight[tap_pos][None, :] * padded[begin : begin + token_count].astype(
            jnp.float32
        )
    active = jax.nn.silu(pre_act)
    blocks = token_count // STRETCH
    grad_heads = upstream.reshape(token_count, head_count, head_size)
    block_idx = 0
    cumulative = jnp.cumsum(decay_rates, axis=0)
    local_parts = [block_product(writes, readers, cumulative, grad_heads)]
    summaries = [block_summary(readers, cumulative, grad_heads)]
    cumulatives = [cumulative]
    device_decay = jnp.ones((head_count,), jnp.float32)
    device_state = jnp.zeros((head_count, state_size, head_size), jnp.float32)
    for block_idx in reversed(range(blocks)):
        device_decay, device_state = later_first(
            (device_decay, device_state),
            (jnp.exp(cumulatives[block_idx][-1]), summaries[block_idx]),
        )
    carried = carried_in((device_decay, device_state), ("seq", "dp"), later_first)
    carry_state = carried[1]
    cumulative = cumulatives[0]
    block_total = cumulative[-1]
    local_part = local_parts[0]
    skip_term = jnp.sum(
        grad_heads.astype(jnp.float32) * active.reshape(token_count, head_count, head_size),
        axis=(0, 2),
    )
    pieces = 4
    head_span = head_count // pieces
    span = head_span * head_size
    passed_parts, weight_parts, bias_parts = [], [], []
    for piece in range(pieces):
        heads = slice(piece * head_span, (piece + 1) * head_span)
        cols = slice(piece * span, (piece + 1) * span)
        carried_part = jnp.einsum(
            "ns,hnp->shp", writes.astype(jnp.float32), carry_state[heads], precision=HIGH
        )
        carried_part = carried_part * jnp.exp(block_total[None, heads] - cumulative[:, heads])[:, :, None]
        grad_act = (
            local_part[:, heads]
            + carried_part
            + skip_row[None, heads, None] * grad_heads[:, heads].astype(jnp.float32)
        )
        grad_pre = grad_act.reshape(token_count, span) * silu_slope(pre_act[:, cols])
        piece_grad, piece_weight, piece_bias = conv_grads(grad_pre, padded[:, cols], weight[:, cols])
        passed_parts.append(from_behind(piece_grad.astype(jnp.bfloat16)[None], "section", -1))
        weight_parts.append(piece_weight)
        bias_parts.append(piece_bias)
    weight_grad = jnp.concatenate(weight_parts, axis=1)
    bias_grad = jnp.concatenate(bias_parts, axis=0)
    group = ("seq", "dp")
    parts = lax.axis_size(group)
    width = channels // parts
    packed = jnp.concatenate(
        [
            weight_grad.reshape(tap_count, parts, width).transpose(1, 0, 2).reshape(parts, tap_count * width),
            bias_grad.reshape(parts, width),
            skip_term.reshape(parts, head_count // parts),
        ],
        axis=1,
    )
    owned = halving_scatter(packed, group)
    shares = (
        owned[: tap_count * width].reshape(tap_count, width),
        owned[tap_count * width : (tap_count + 1) * width],
        owned[(tap_count + 1) * width :],
    )
    passed = jnp.concatenate(passed_parts, axis=2)
    return (passed, shares[0][None], shares[1][None], shares[2][None])


def solution(mesh):
    placed = (
        P("section", ("seq", "dp"), None),
        P("section", None, None),
        P("section", None),
        P("section", ("seq", "dp"), None),
        P("section", None, ("seq", "dp")),
        P("section", None, ("seq", "dp")),
        P("section", None),
        P("section", ("seq", "dp"), None),
    )
    return jax.shard_map(
        on_device,
        mesh=mesh,
        in_specs=placed,
        out_specs=(
            P("section", ("seq", "dp"), None),
            P("section", None, ("seq", "dp")),
            P("section", ("seq", "dp")),
            P("section", ("seq", "dp")),
        ),
        check_vma=False,
    )
```

```python
import jax
import jax.numpy as jnp
from jax import lax
from jax.sharding import PartitionSpec as P

STRETCH = 256


HIGH = lax.Precision.HIGHEST
group_heads = 32


def from_behind(block, axis, distance):
    devices = range(lax.axis_size(axis))
    route = [(i - distance, i) for i in devices if i - distance in devices]
    return lax.ppermute(block, axis, route)


def shifted_from(part, axis, distance):
    count = lax.axis_size(axis)
    route = [(i + distance, i) for i in range(count) if i + distance < count]
    return jax.tree.map(lambda a: narrow_ppermute(a, axis, route), part)


def narrow_ppermute(a, axis, route):
    if a.ndim < 3:
        return lax.ppermute(a, axis, route)
    return lax.ppermute(a.astype(jnp.bfloat16), axis, route).astype(a.dtype)


def carried_in(part, axis, combine):
    count = lax.axis_size(axis)
    state = shifted_from(part, axis, 1)
    distance = 1
    while distance < count - 1:
        state = combine(shifted_from(state, axis, distance), state)
        distance *= 2
    return state


def halving_scatter(rows, axis):
    count = lax.axis_size(axis)
    place = lax.axis_index(axis)
    mask = count // 2
    while mask >= 1:
        pairs = rows.reshape((2, rows.shape[0] // 2) + rows.shape[1:])
        upper = (place // mask) % 2 == 1
        keep = jnp.where(upper, pairs[1], pairs[0])
        send = jnp.where(upper, pairs[0], pairs[1])
        route = [(i, i ^ mask) for i in range(count)]
        rows = keep + lax.ppermute(send, axis, route)
        mask //= 2
    return rows[0]


def silu_slope(pre_act):
    sigma = jax.nn.sigmoid(pre_act)
    return sigma * (1.0 + pre_act * (1.0 - sigma))


def later_first(earlier, later):
    decay_high, state_high = earlier
    decay_low, state_low = later
    return (decay_low * decay_high, state_low + decay_low[:, None, None] * state_high)


def block_product(writes, readers, cumulative, upstream):
    scores = lax.dot_general(
        writes, readers, (((0,), (0,)), ((), ())), preferred_element_type=jnp.float32
    )
    span_len = scores.shape[0]
    row_ids = lax.broadcasted_iota(jnp.int32, (span_len, span_len), 0)
    col_ids = lax.broadcasted_iota(jnp.int32, (span_len, span_len), 1)
    causal = col_ids >= row_ids
    head_count = cumulative.shape[1]
    group_size = min(group_heads, head_count)
    pieces = []
    for first_head in range(0, head_count, group_size):
        head_rates = cumulative[:, first_head : first_head + group_size].T
        spread = head_rates[:, None, :] - head_rates[:, :, None]
        weights = jnp.where(
            causal[None], jnp.exp(jnp.minimum(spread, 0.0)) * scores[None], 0.0
        ).astype(jnp.bfloat16)
        pieces.append(
            jnp.einsum(
                "hst,thp->shp",
                weights,
                upstream[:, first_head : first_head + group_size, :],
                preferred_element_type=jnp.float32,
            )
        )
    return jnp.concatenate(pieces, axis=1)


def block_summary(readers, cumulative, upstream):
    weighted = (readers.astype(jnp.float32)[None, :, :] * jnp.exp(cumulative).T[:, None, :]).astype(
        jnp.bfloat16
    )
    return jnp.einsum("hnt,thp->hnp", weighted, upstream, preferred_element_type=jnp.float32)


def conv_grads(grad_pre, padded, weight):
    token_count = grad_pre.shape[0]
    tap_count = weight.shape[0]
    after_rows = from_behind(grad_pre[: tap_count - 1], ("seq", "dp"), -1)
    extended = jnp.concatenate([grad_pre, after_rows], axis=0)
    input_grad = jnp.zeros(grad_pre.shape, jnp.float32)
    weight_terms = []
    for tap_pos in range(tap_count):
        input_grad = (
            input_grad + weight[tap_pos][None, :] * extended[tap_pos : tap_pos + token_count]
        )
        begin = tap_count - 1 - tap_pos
        weight_terms.append(
            jnp.sum(grad_pre * padded[begin : begin + token_count].astype(jnp.float32), axis=0)
        )
    return input_grad, jnp.stack(weight_terms, axis=0), jnp.sum(grad_pre, axis=0)


def on_device(
    layer_input, conv_weight, conv_bias, log_decay, state_write, state_read, skip_gain, grad_out
):
    inputs = layer_input[0]
    weight = conv_weight[0]
    bias_row = conv_bias[0]
    decay_rates = log_decay[0]
    writes = state_write[0]
    readers = state_read[0]
    skip_row = skip_gain[0]
    upstream = grad_out[0]
    token_count, channels = inputs.shape
    head_count = decay_rates.shape[1]
    head_size = channels // head_count
    state_size = writes.shape[0]
    tap_count = weight.shape[0]
    prior_rows = from_behind(inputs[token_count - (tap_count - 1) :], ("seq", "dp"), 1)
    padded = jnp.concatenate([prior_rows, inputs], axis=0)
    pre_act = jnp.broadcast_to(bias_row[None, :], (token_count, channels))
    for tap_pos in range(tap_count):
        begin = tap_count - 1 - tap_pos
        pre_act = pre_act + weight[tap_pos][None, :] * padded[begin : begin + token_count].astype(
            jnp.float32
        )
    active = jax.nn.silu(pre_act)
    blocks = token_count // STRETCH
    grad_heads = upstream.reshape(token_count, head_count, head_size)
    block_idx = 0
    cumulative = jnp.cumsum(decay_rates, axis=0)
    local_parts = [block_product(writes, readers, cumulative, grad_heads)]
    summaries = [block_summary(readers, cumulative, grad_heads)]
    cumulatives = [cumulative]
    device_decay = jnp.ones((head_count,), jnp.float32)
    device_state = jnp.zeros((head_count, state_size, head_size), jnp.float32)
    for block_idx in reversed(range(blocks)):
        device_decay, device_state = later_first(
            (device_decay, device_state),
            (jnp.exp(cumulatives[block_idx][-1]), summaries[block_idx]),
        )
    carried = carried_in((device_decay, device_state), ("seq", "dp"), later_first)
    carry_state = carried[1]
    cumulative = cumulatives[0]
    block_total = cumulative[-1]
    local_part = local_parts[0]
    skip_term = jnp.sum(
        grad_heads.astype(jnp.float32) * active.reshape(token_count, head_count, head_size),
        axis=(0, 2),
    )
    pieces = 4
    head_span = head_count // pieces
    span = head_span * head_size
    passed_parts, weight_parts, bias_parts = [], [], []
    for piece in range(pieces):
        heads = slice(piece * head_span, (piece + 1) * head_span)
        cols = slice(piece * span, (piece + 1) * span)
        carried_part = jnp.einsum(
            "ns,hnp->shp", writes.astype(jnp.float32), carry_state[heads], precision=HIGH
        )
        carried_part = carried_part * jnp.exp(block_total[None, heads] - cumulative[:, heads])[:, :, None]
        grad_act = (
            local_part[:, heads]
            + carried_part
            + skip_row[None, heads, None] * grad_heads[:, heads].astype(jnp.float32)
        )
        grad_pre = grad_act.reshape(token_count, span) * silu_slope(pre_act[:, cols])
        piece_grad, piece_weight, piece_bias = conv_grads(grad_pre, padded[:, cols], weight[:, cols])
        passed_parts.append(from_behind(piece_grad.astype(jnp.bfloat16)[None], "section", -1))
        weight_parts.append(piece_weight)
        bias_parts.append(piece_bias)
    weight_grad = jnp.concatenate(weight_parts, axis=1)
    bias_grad = jnp.concatenate(bias_parts, axis=0)
    group = ("seq", "dp")
    parts = lax.axis_size(group)
    width = channels // parts
    packed = jnp.concatenate(
        [
            weight_grad.reshape(tap_count, parts, width).transpose(1, 0, 2).reshape(parts, tap_count * width),
            bias_grad.reshape(parts, width),
            skip_term.reshape(parts, head_count // parts),
        ],
        axis=1,
    )
    owned = halving_scatter(packed, group)
    shares = (
        owned[: tap_count * width].reshape(tap_count, width),
        owned[tap_count * width : (tap_count + 1) * width],
        owned[(tap_count + 1) * width :],
    )
    passed = jnp.concatenate(passed_parts, axis=2)
    return (passed, shares[0][None], shares[1][None], shares[2][None])


def solution(mesh):
    placed = (
        P("section", ("seq", "dp"), None),
        P("section", None, None),
        P("section", None),
        P("section", ("seq", "dp"), None),
        P("section", None, ("seq", "dp")),
        P("section", None, ("seq", "dp")),
        P("section", None),
        P("section", ("seq", "dp"), None),
    )
    return jax.shard_map(
        on_device,
        mesh=mesh,
        in_specs=placed,
        out_specs=(
            P("section", ("seq", "dp"), None),
            P("section", None, ("seq", "dp")),
            P("section", ("seq", "dp")),
            P("section", ("seq", "dp")),
        ),
        check_vma=False,
    )
```

```python
import jax
import jax.numpy as jnp
from jax import lax
from jax.sharding import PartitionSpec as P

STRETCH = 256


HIGH = lax.Precision.HIGHEST
group_heads = 32


def from_behind(block, axis, distance):
    devices = range(lax.axis_size(axis))
    route = [(i - distance, i) for i in devices if i - distance in devices]
    return lax.ppermute(block, axis, route)


def shifted_from(part, axis, distance):
    count = lax.axis_size(axis)
    route = [(i + distance, i) for i in range(count) if i + distance < count]
    return jax.tree.map(lambda a: narrow_ppermute(a, axis, route), part)


def narrow_ppermute(a, axis, route):
    if a.ndim < 3:
        return lax.ppermute(a, axis, route)
    return lax.ppermute(a.astype(jnp.bfloat16), axis, route).astype(a.dtype)


def carried_in(part, axis, combine):
    count = lax.axis_size(axis)
    state = shifted_from(part, axis, 1)
    distance = 1
    while distance < count - 1:
        state = combine(shifted_from(state, axis, distance), state)
        distance *= 2
    return state


def halving_scatter(rows, axis):
    count = lax.axis_size(axis)
    place = lax.axis_index(axis)
    mask = count // 2
    while mask >= 1:
        pairs = rows.reshape((2, rows.shape[0] // 2) + rows.shape[1:])
        upper = (place // mask) % 2 == 1
        keep = jnp.where(upper, pairs[1], pairs[0])
        send = jnp.where(upper, pairs[0], pairs[1])
        route = [(i, i ^ mask) for i in range(count)]
        rows = keep + lax.ppermute(send, axis, route)
        mask //= 2
    return rows[0]


def silu_slope(pre_act):
    sigma = jax.nn.sigmoid(pre_act)
    return sigma * (1.0 + pre_act * (1.0 - sigma))


def later_first(earlier, later):
    decay_high, state_high = earlier
    decay_low, state_low = later
    return (decay_low * decay_high, state_low + decay_low[:, None, None] * state_high)


def block_product(writes, readers, cumulative, upstream):
    scores = lax.dot_general(
        writes, readers, (((0,), (0,)), ((), ())), preferred_element_type=jnp.float32
    )
    span_len = scores.shape[0]
    row_ids = lax.broadcasted_iota(jnp.int32, (span_len, span_len), 0)
    col_ids = lax.broadcasted_iota(jnp.int32, (span_len, span_len), 1)
    causal = col_ids >= row_ids
    head_count = cumulative.shape[1]
    group_size = min(group_heads, head_count)
    pieces = []
    for first_head in range(0, head_count, group_size):
        head_rates = cumulative[:, first_head : first_head + group_size].T
        spread = head_rates[:, None, :] - head_rates[:, :, None]
        weights = jnp.where(
            causal[None], jnp.exp(jnp.minimum(spread, 0.0)) * scores[None], 0.0
        ).astype(jnp.bfloat16)
        pieces.append(
            jnp.einsum(
                "hst,thp->shp",
                weights,
                upstream[:, first_head : first_head + group_size, :],
                preferred_element_type=jnp.float32,
            )
        )
    return jnp.concatenate(pieces, axis=1)


def block_summary(readers, cumulative, upstream):
    weighted = (readers.astype(jnp.float32)[None, :, :] * jnp.exp(cumulative).T[:, None, :]).astype(
        jnp.bfloat16
    )
    return jnp.einsum("hnt,thp->hnp", weighted, upstream, preferred_element_type=jnp.float32)


def conv_grads(grad_pre, padded, weight):
    token_count = grad_pre.shape[0]
    tap_count = weight.shape[0]
    after_rows = from_behind(grad_pre[: tap_count - 1], ("seq", "dp"), -1)
    extended = jnp.concatenate([grad_pre, after_rows], axis=0)
    input_grad = jnp.zeros(grad_pre.shape, jnp.float32)
    weight_terms = []
    for tap_pos in range(tap_count):
        input_grad = (
            input_grad + weight[tap_pos][None, :] * extended[tap_pos : tap_pos + token_count]
        )
        begin = tap_count - 1 - tap_pos
        weight_terms.append(
            jnp.sum(grad_pre * padded[begin : begin + token_count].astype(jnp.float32), axis=0)
        )
    return input_grad, jnp.stack(weight_terms, axis=0), jnp.sum(grad_pre, axis=0)


def on_device(
    layer_input, conv_weight, conv_bias, log_decay, state_write, state_read, skip_gain, grad_out
):
    inputs = layer_input[0]
    weight = conv_weight[0]
    bias_row = conv_bias[0]
    decay_rates = log_decay[0]
    writes = state_write[0]
    readers = state_read[0]
    skip_row = skip_gain[0]
    upstream = grad_out[0]
    token_count, channels = inputs.shape
    head_count = decay_rates.shape[1]
    head_size = channels // head_count
    state_size = writes.shape[0]
    tap_count = weight.shape[0]
    prior_rows = from_behind(inputs[token_count - (tap_count - 1) :], ("seq", "dp"), 1)
    padded = jnp.concatenate([prior_rows, inputs], axis=0)
    pre_act = jnp.broadcast_to(bias_row[None, :], (token_count, channels))
    for tap_pos in range(tap_count):
        begin = tap_count - 1 - tap_pos
        pre_act = pre_act + weight[tap_pos][None, :] * padded[begin : begin + token_count].astype(
            jnp.float32
        )
    active = jax.nn.silu(pre_act)
    blocks = token_count // STRETCH
    grad_heads = upstream.reshape(token_count, head_count, head_size)
    block_idx = 0
    cumulative = jnp.cumsum(decay_rates, axis=0)
    local_parts = [block_product(writes, readers, cumulative, grad_heads)]
    summaries = [block_summary(readers, cumulative, grad_heads)]
    cumulatives = [cumulative]
    device_decay = jnp.ones((head_count,), jnp.float32)
    device_state = jnp.zeros((head_count, state_size, head_size), jnp.float32)
    for block_idx in reversed(range(blocks)):
        device_decay, device_state = later_first(
            (device_decay, device_state),
            (jnp.exp(cumulatives[block_idx][-1]), summaries[block_idx]),
        )
    carried = carried_in((device_decay, device_state), ("seq", "dp"), later_first)
    carry_state = carried[1]
    cumulative = cumulatives[0]
    block_total = cumulative[-1]
    local_part = local_parts[0]
    skip_term = jnp.sum(
        grad_heads.astype(jnp.float32) * active.reshape(token_count, head_count, head_size),
        axis=(0, 2),
    )
    pieces = 4
    head_span = head_count // pieces
    span = head_span * head_size
    passed_parts, weight_parts, bias_parts = [], [], []
    for piece in range(pieces):
        heads = slice(piece * head_span, (piece + 1) * head_span)
        cols = slice(piece * span, (piece + 1) * span)
        piece_local, piece_upstream, piece_padded = local_part[:, heads], grad_heads[:, heads], padded[:, cols]
        if piece:
            after = passed_parts[piece - 2] if piece >= 2 else previous
            piece_local, piece_upstream, piece_padded, _ = lax.optimization_barrier(
                (piece_local, piece_upstream, piece_padded, after)
            )
        carried_part = jnp.einsum(
            "ns,hnp->shp", writes.astype(jnp.float32), carry_state[heads], precision=HIGH
        )
        carried_part = carried_part * jnp.exp(block_total[None, heads] - cumulative[:, heads])[:, :, None]
        grad_act = (
            piece_local
            + carried_part
            + skip_row[None, heads, None] * piece_upstream.astype(jnp.float32)
        )
        piece_pre = jnp.broadcast_to(bias_row[None, cols], (token_count, span))
        for tap_pos in range(tap_count):
            begin = tap_count - 1 - tap_pos
            piece_pre = piece_pre + weight[tap_pos][None, cols] * piece_padded[
                begin : begin + token_count
            ].astype(jnp.float32)
        grad_pre = grad_act.reshape(token_count, span) * silu_slope(piece_pre)
        piece_grad, piece_weight, piece_bias = conv_grads(grad_pre, piece_padded, weight[:, cols])
        previous = piece_grad.astype(jnp.bfloat16)
        passed_parts.append(from_behind(previous[None], "section", -1))
        weight_parts.append(piece_weight)
        bias_parts.append(piece_bias)
    weight_grad = jnp.concatenate(weight_parts, axis=1)
    bias_grad = jnp.concatenate(bias_parts, axis=0)
    group = ("seq", "dp")
    parts = lax.axis_size(group)
    width = channels // parts
    packed = jnp.concatenate(
        [
            weight_grad.reshape(tap_count, parts, width).transpose(1, 0, 2).reshape(parts, tap_count * width),
            bias_grad.reshape(parts, width),
            skip_term.reshape(parts, head_count // parts),
        ],
        axis=1,
    )
    owned = halving_scatter(packed, group)
    shares = (
        owned[: tap_count * width].reshape(tap_count, width),
        owned[tap_count * width : (tap_count + 1) * width],
        owned[(tap_count + 1) * width :],
    )
    passed = jnp.concatenate(passed_parts, axis=2)
    return (passed, shares[0][None], shares[1][None], shares[2][None])


def solution(mesh):
    placed = (
        P("section", ("seq", "dp"), None),
        P("section", None, None),
        P("section", None),
        P("section", ("seq", "dp"), None),
        P("section", None, ("seq", "dp")),
        P("section", None, ("seq", "dp")),
        P("section", None),
        P("section", ("seq", "dp"), None),
    )
    return jax.shard_map(
        on_device,
        mesh=mesh,
        in_specs=placed,
        out_specs=(
            P("section", ("seq", "dp"), None),
            P("section", None, ("seq", "dp")),
            P("section", ("seq", "dp")),
            P("section", ("seq", "dp")),
        ),
        check_vma=False,
    )
```

```python
import jax
import jax.numpy as jnp
from jax import lax
from jax.sharding import PartitionSpec as P

STRETCH = 256


HIGH = lax.Precision.HIGHEST
group_heads = 32


def from_behind(block, axis, distance):
    devices = range(lax.axis_size(axis))
    route = [(i - distance, i) for i in devices if i - distance in devices]
    return lax.ppermute(block, axis, route)


def shifted_from(part, axis, distance):
    count = lax.axis_size(axis)
    route = [(i + distance, i) for i in range(count) if i + distance < count]
    return jax.tree.map(lambda a: narrow_ppermute(a, axis, route), part)


def narrow_ppermute(a, axis, route):
    if a.ndim < 3:
        return lax.ppermute(a, axis, route)
    return lax.ppermute(a.astype(jnp.bfloat16), axis, route).astype(a.dtype)


def carried_in(part, axis, combine):
    count = lax.axis_size(axis)
    state = shifted_from(part, axis, 1)
    distance = 1
    while distance < count - 1:
        state = combine(shifted_from(state, axis, distance), state)
        distance *= 2
    return state


def halving_scatter(rows, axis):
    count = lax.axis_size(axis)
    place = lax.axis_index(axis)
    mask = 1
    while mask < count:
        pairs = rows.reshape((rows.shape[0] // 2, 2) + rows.shape[1:])
        upper = (place // mask) % 2 == 1
        keep = jnp.where(upper, pairs[:, 1], pairs[:, 0])
        send = jnp.where(upper, pairs[:, 0], pairs[:, 1])
        route = [(i, i ^ mask) for i in range(count)]
        rows = keep + lax.ppermute(send, axis, route)
        mask *= 2
    return rows[0]


def silu_slope(pre_act):
    sigma = jax.nn.sigmoid(pre_act)
    return sigma * (1.0 + pre_act * (1.0 - sigma))


def later_first(earlier, later):
    decay_high, state_high = earlier
    decay_low, state_low = later
    return (decay_low * decay_high, state_low + decay_low[:, None, None] * state_high)


def block_product(writes, readers, cumulative, upstream):
    scores = lax.dot_general(
        writes, readers, (((0,), (0,)), ((), ())), preferred_element_type=jnp.float32
    )
    span_len = scores.shape[0]
    row_ids = lax.broadcasted_iota(jnp.int32, (span_len, span_len), 0)
    col_ids = lax.broadcasted_iota(jnp.int32, (span_len, span_len), 1)
    causal = col_ids >= row_ids
    head_count = cumulative.shape[1]
    group_size = min(group_heads, head_count)
    pieces = []
    for first_head in range(0, head_count, group_size):
        head_rates = cumulative[:, first_head : first_head + group_size].T
        spread = head_rates[:, None, :] - head_rates[:, :, None]
        weights = jnp.where(
            causal[None], jnp.exp(jnp.minimum(spread, 0.0)) * scores[None], 0.0
        ).astype(jnp.bfloat16)
        pieces.append(
            jnp.einsum(
                "hst,thp->shp",
                weights,
                upstream[:, first_head : first_head + group_size, :],
                preferred_element_type=jnp.float32,
            )
        )
    return jnp.concatenate(pieces, axis=1)


def block_summary(readers, cumulative, upstream):
    weighted = (readers.astype(jnp.float32)[None, :, :] * jnp.exp(cumulative).T[:, None, :]).astype(
        jnp.bfloat16
    )
    return jnp.einsum("hnt,thp->hnp", weighted, upstream, preferred_element_type=jnp.float32)


def conv_grads(grad_pre, padded, weight):
    token_count = grad_pre.shape[0]
    tap_count = weight.shape[0]
    after_rows = from_behind(grad_pre[: tap_count - 1], ("seq", "dp"), -1)
    extended = jnp.concatenate([grad_pre, after_rows], axis=0)
    input_grad = jnp.zeros(grad_pre.shape, jnp.float32)
    weight_terms = []
    for tap_pos in range(tap_count):
        input_grad = (
            input_grad + weight[tap_pos][None, :] * extended[tap_pos : tap_pos + token_count]
        )
        begin = tap_count - 1 - tap_pos
        weight_terms.append(
            jnp.sum(grad_pre * padded[begin : begin + token_count].astype(jnp.float32), axis=0)
        )
    return input_grad, jnp.stack(weight_terms, axis=0), jnp.sum(grad_pre, axis=0)


def on_device(
    layer_input, conv_weight, conv_bias, log_decay, state_write, state_read, skip_gain, grad_out
):
    inputs = layer_input[0]
    weight = conv_weight[0]
    bias_row = conv_bias[0]
    decay_rates = log_decay[0]
    writes = state_write[0]
    readers = state_read[0]
    skip_row = skip_gain[0]
    upstream = grad_out[0]
    token_count, channels = inputs.shape
    head_count = decay_rates.shape[1]
    head_size = channels // head_count
    state_size = writes.shape[0]
    tap_count = weight.shape[0]
    prior_rows = from_behind(inputs[token_count - (tap_count - 1) :], ("seq", "dp"), 1)
    padded = jnp.concatenate([prior_rows, inputs], axis=0)
    pre_act = jnp.broadcast_to(bias_row[None, :], (token_count, channels))
    for tap_pos in range(tap_count):
        begin = tap_count - 1 - tap_pos
        pre_act = pre_act + weight[tap_pos][None, :] * padded[begin : begin + token_count].astype(
            jnp.float32
        )
    active = jax.nn.silu(pre_act)
    blocks = token_count // STRETCH
    grad_heads = upstream.reshape(token_count, head_count, head_size)
    block_idx = 0
    cumulative = jnp.cumsum(decay_rates, axis=0)
    local_parts = [block_product(writes, readers, cumulative, grad_heads)]
    summaries = [block_summary(readers, cumulative, grad_heads)]
    cumulatives = [cumulative]
    device_decay = jnp.ones((head_count,), jnp.float32)
    device_state = jnp.zeros((head_count, state_size, head_size), jnp.float32)
    for block_idx in reversed(range(blocks)):
        device_decay, device_state = later_first(
            (device_decay, device_state),
            (jnp.exp(cumulatives[block_idx][-1]), summaries[block_idx]),
        )
    carried = carried_in((device_decay, device_state), ("seq", "dp"), later_first)
    carry_state = carried[1]
    cumulative = cumulatives[0]
    block_total = cumulative[-1]
    local_part = local_parts[0]
    skip_term = jnp.sum(
        grad_heads.astype(jnp.float32) * active.reshape(token_count, head_count, head_size),
        axis=(0, 2),
    )
    pieces = 4
    head_span = head_count // pieces
    span = head_span * head_size
    passed_parts, weight_parts, bias_parts = [], [], []
    for piece in range(pieces):
        heads = slice(piece * head_span, (piece + 1) * head_span)
        cols = slice(piece * span, (piece + 1) * span)
        piece_local, piece_upstream, piece_padded = local_part[:, heads], grad_heads[:, heads], padded[:, cols]
        if piece:
            after = passed_parts[piece - 2] if piece >= 2 else previous
            piece_local, piece_upstream, piece_padded, _ = lax.optimization_barrier(
                (piece_local, piece_upstream, piece_padded, after)
            )
        carried_part = jnp.einsum(
            "ns,hnp->shp", writes.astype(jnp.float32), carry_state[heads], precision=HIGH
        )
        carried_part = carried_part * jnp.exp(block_total[None, heads] - cumulative[:, heads])[:, :, None]
        grad_act = (
            piece_local
            + carried_part
            + skip_row[None, heads, None] * piece_upstream.astype(jnp.float32)
        )
        piece_pre = jnp.broadcast_to(bias_row[None, cols], (token_count, span))
        for tap_pos in range(tap_count):
            begin = tap_count - 1 - tap_pos
            piece_pre = piece_pre + weight[tap_pos][None, cols] * piece_padded[
                begin : begin + token_count
            ].astype(jnp.float32)
        grad_pre = grad_act.reshape(token_count, span) * silu_slope(piece_pre)
        piece_grad, piece_weight, piece_bias = conv_grads(grad_pre, piece_padded, weight[:, cols])
        previous = piece_grad.astype(jnp.bfloat16)
        passed_parts.append(from_behind(previous[None], "section", -1))
        weight_parts.append(piece_weight)
        bias_parts.append(piece_bias)
    weight_grad = jnp.concatenate(weight_parts, axis=1)
    bias_grad = jnp.concatenate(bias_parts, axis=0)
    group = ("seq", "dp")
    parts = lax.axis_size(group)
    width = channels // parts
    packed = jnp.concatenate(
        [
            weight_grad.reshape(tap_count, parts, width).transpose(1, 0, 2).reshape(parts, tap_count * width),
            bias_grad.reshape(parts, width),
            skip_term.reshape(parts, head_count // parts),
        ],
        axis=1,
    )
    owned = halving_scatter(packed, group)
    shares = (
        owned[: tap_count * width].reshape(tap_count, width),
        owned[tap_count * width : (tap_count + 1) * width],
        owned[(tap_count + 1) * width :],
    )
    passed = jnp.concatenate(passed_parts, axis=2)
    return (passed, shares[0][None], shares[1][None], shares[2][None])


def solution(mesh):
    placed = (
        P("section", ("seq", "dp"), None),
        P("section", None, None),
        P("section", None),
        P("section", ("seq", "dp"), None),
        P("section", None, ("seq", "dp")),
        P("section", None, ("seq", "dp")),
        P("section", None),
        P("section", ("seq", "dp"), None),
    )
    return jax.shard_map(
        on_device,
        mesh=mesh,
        in_specs=placed,
        out_specs=(
            P("section", ("seq", "dp"), None),
            P("section", None, ("seq", "dp")),
            P("section", ("seq", "dp")),
            P("section", ("seq", "dp")),
        ),
        check_vma=False,
    )
```

```python
import jax
import jax.numpy as jnp
from jax import lax
from jax.sharding import PartitionSpec as P

STRETCH = 256


HIGH = lax.Precision.HIGHEST
group_heads = 32


def from_behind(block, axis, distance):
    devices = range(lax.axis_size(axis))
    route = [(i - distance, i) for i in devices if i - distance in devices]
    return lax.ppermute(block, axis, route)


def shifted_from(part, axis, distance):
    count = lax.axis_size(axis)
    route = [(i + distance, i) for i in range(count) if i + distance < count]
    return jax.tree.map(lambda a: lax.ppermute(a, axis, route), part)


def carried_in(part, axis, combine):
    count = lax.axis_size(axis)
    state = shifted_from(part, axis, 1)
    distance = 1
    while distance < count - 1:
        state = combine(shifted_from(state, axis, distance), state)
        distance *= 2
    return state


def halving_scatter(rows, axis):
    count = lax.axis_size(axis)
    place = lax.axis_index(axis)
    mask = count // 2
    while mask >= 1:
        pairs = rows.reshape((2, rows.shape[0] // 2) + rows.shape[1:])
        upper = (place // mask) % 2 == 1
        keep = jnp.where(upper, pairs[1], pairs[0])
        send = jnp.where(upper, pairs[0], pairs[1])
        route = [(i, i ^ mask) for i in range(count)]
        rows = keep + lax.ppermute(send, axis, route)
        mask //= 2
    return rows[0]


def silu_slope(pre_act):
    sigma = jax.nn.sigmoid(pre_act)
    return sigma * (1.0 + pre_act * (1.0 - sigma))


def later_first(earlier, later):
    decay_high, state_high = earlier
    decay_low, state_low = later
    return (decay_low * decay_high, state_low + decay_low[:, None, None] * state_high)


def block_product(writes, readers, cumulative, upstream):
    scores = lax.dot_general(
        writes, readers, (((0,), (0,)), ((), ())), preferred_element_type=jnp.float32
    )
    span_len = scores.shape[0]
    row_ids = lax.broadcasted_iota(jnp.int32, (span_len, span_len), 0)
    col_ids = lax.broadcasted_iota(jnp.int32, (span_len, span_len), 1)
    causal = col_ids >= row_ids
    head_count = cumulative.shape[1]
    group_size = min(group_heads, head_count)
    pieces = []
    for first_head in range(0, head_count, group_size):
        head_rates = cumulative[:, first_head : first_head + group_size].T
        spread = head_rates[:, None, :] - head_rates[:, :, None]
        weights = jnp.where(
            causal[None], jnp.exp(jnp.minimum(spread, 0.0)) * scores[None], 0.0
        ).astype(jnp.bfloat16)
        pieces.append(
            jnp.einsum(
                "hst,thp->shp",
                weights,
                upstream[:, first_head : first_head + group_size, :],
                preferred_element_type=jnp.float32,
            )
        )
    return jnp.concatenate(pieces, axis=1)


def block_summary(readers, cumulative, upstream):
    weighted = (readers.astype(jnp.float32)[None, :, :] * jnp.exp(cumulative).T[:, None, :]).astype(
        jnp.bfloat16
    )
    return jnp.einsum("hnt,thp->hnp", weighted, upstream, preferred_element_type=jnp.float32)


def conv_grads(grad_pre, padded, weight):
    token_count = grad_pre.shape[0]
    tap_count = weight.shape[0]
    after_rows = from_behind(grad_pre[: tap_count - 1], ("seq", "dp"), -1)
    extended = jnp.concatenate([grad_pre, after_rows], axis=0)
    input_grad = jnp.zeros(grad_pre.shape, jnp.float32)
    weight_terms = []
    for tap_pos in range(tap_count):
        input_grad = (
            input_grad + weight[tap_pos][None, :] * extended[tap_pos : tap_pos + token_count]
        )
        begin = tap_count - 1 - tap_pos
        weight_terms.append(
            jnp.sum(grad_pre * padded[begin : begin + token_count].astype(jnp.float32), axis=0)
        )
    return input_grad, jnp.stack(weight_terms, axis=0), jnp.sum(grad_pre, axis=0)


def on_device(
    layer_input, conv_weight, conv_bias, log_decay, state_write, state_read, skip_gain, grad_out
):
    inputs = layer_input[0]
    weight = conv_weight[0]
    bias_row = conv_bias[0]
    decay_rates = log_decay[0]
    writes = state_write[0]
    readers = state_read[0]
    skip_row = skip_gain[0]
    upstream = grad_out[0]
    token_count, channels = inputs.shape
    head_count = decay_rates.shape[1]
    head_size = channels // head_count
    state_size = writes.shape[0]
    tap_count = weight.shape[0]
    prior_rows = from_behind(inputs[token_count - (tap_count - 1) :], ("seq", "dp"), 1)
    padded = jnp.concatenate([prior_rows, inputs], axis=0)
    pre_act = jnp.broadcast_to(bias_row[None, :], (token_count, channels))
    for tap_pos in range(tap_count):
        begin = tap_count - 1 - tap_pos
        pre_act = pre_act + weight[tap_pos][None, :] * padded[begin : begin + token_count].astype(
            jnp.float32
        )
    active = jax.nn.silu(pre_act)
    blocks = token_count // STRETCH
    grad_heads = upstream.reshape(token_count, head_count, head_size)
    block_idx = 0
    cumulative = jnp.cumsum(decay_rates, axis=0)
    local_parts = [block_product(writes, readers, cumulative, grad_heads)]
    summaries = [block_summary(readers, cumulative, grad_heads)]
    cumulatives = [cumulative]
    device_decay = jnp.ones((head_count,), jnp.float32)
    device_state = jnp.zeros((head_count, state_size, head_size), jnp.float32)
    for block_idx in reversed(range(blocks)):
        device_decay, device_state = later_first(
            (device_decay, device_state),
            (jnp.exp(cumulatives[block_idx][-1]), summaries[block_idx]),
        )
    carried = carried_in((device_decay, device_state), ("seq", "dp"), later_first)
    carry_state = carried[1]
    cumulative = cumulatives[0]
    block_total = cumulative[-1]
    local_part = local_parts[0]
    skip_term = jnp.sum(
        grad_heads.astype(jnp.float32) * active.reshape(token_count, head_count, head_size),
        axis=(0, 2),
    )
    pieces = 4
    head_span = head_count // pieces
    span = head_span * head_size
    passed_parts, weight_parts, bias_parts = [], [], []
    for piece in range(pieces):
        heads = slice(piece * head_span, (piece + 1) * head_span)
        cols = slice(piece * span, (piece + 1) * span)
        piece_local, piece_upstream, piece_padded = local_part[:, heads], grad_heads[:, heads], padded[:, cols]
        if piece:
            after = passed_parts[piece - 2] if piece >= 2 else previous
            piece_local, piece_upstream, piece_padded, _ = lax.optimization_barrier(
                (piece_local, piece_upstream, piece_padded, after)
            )
        carried_part = jnp.einsum(
            "ns,hnp->shp", writes.astype(jnp.float32), carry_state[heads], precision=HIGH
        )
        carried_part = carried_part * jnp.exp(block_total[None, heads] - cumulative[:, heads])[:, :, None]
        grad_act = (
            piece_local
            + carried_part
            + skip_row[None, heads, None] * piece_upstream.astype(jnp.float32)
        )
        piece_pre = jnp.broadcast_to(bias_row[None, cols], (token_count, span))
        for tap_pos in range(tap_count):
            begin = tap_count - 1 - tap_pos
            piece_pre = piece_pre + weight[tap_pos][None, cols] * piece_padded[
                begin : begin + token_count
            ].astype(jnp.float32)
        grad_pre = grad_act.reshape(token_count, span) * silu_slope(piece_pre)
        piece_grad, piece_weight, piece_bias = conv_grads(grad_pre, piece_padded, weight[:, cols])
        previous = piece_grad.astype(jnp.bfloat16)
        passed_parts.append(from_behind(previous[None], "section", -1))
        weight_parts.append(piece_weight)
        bias_parts.append(piece_bias)
    weight_grad = jnp.concatenate(weight_parts, axis=1)
    bias_grad = jnp.concatenate(bias_parts, axis=0)
    group = ("seq", "dp")
    parts = lax.axis_size(group)
    width = channels // parts
    packed = jnp.concatenate(
        [
            weight_grad.reshape(tap_count, parts, width).transpose(1, 0, 2).reshape(parts, tap_count * width),
            bias_grad.reshape(parts, width),
            skip_term.reshape(parts, head_count // parts),
        ],
        axis=1,
    )
    owned = halving_scatter(packed, group)
    shares = (
        owned[: tap_count * width].reshape(tap_count, width),
        owned[tap_count * width : (tap_count + 1) * width],
        owned[(tap_count + 1) * width :],
    )
    passed = jnp.concatenate(passed_parts, axis=2)
    return (passed, shares[0][None], shares[1][None], shares[2][None])


def solution(mesh):
    placed = (
        P("section", ("seq", "dp"), None),
        P("section", None, None),
        P("section", None),
        P("section", ("seq", "dp"), None),
        P("section", None, ("seq", "dp")),
        P("section", None, ("seq", "dp")),
        P("section", None),
        P("section", ("seq", "dp"), None),
    )
    return jax.shard_map(
        on_device,
        mesh=mesh,
        in_specs=placed,
        out_specs=(
            P("section", ("seq", "dp"), None),
            P("section", None, ("seq", "dp")),
            P("section", ("seq", "dp")),
            P("section", ("seq", "dp")),
        ),
        check_vma=False,
    )
```

```python
import jax
import jax.numpy as jnp
from jax import lax
from jax.sharding import PartitionSpec as P

STRETCH = 256


HIGH = lax.Precision.HIGHEST
group_heads = 32


def from_behind(block, axis, distance):
    devices = range(lax.axis_size(axis))
    route = [(i - distance, i) for i in devices if i - distance in devices]
    return lax.ppermute(block, axis, route)


def shifted_from(part, axis, distance):
    count = lax.axis_size(axis)
    route = [(i + distance, i) for i in range(count) if i + distance < count]
    return jax.tree.map(lambda a: lax.ppermute(a, axis, route), part)


def carried_in(part, axis, combine):
    count = lax.axis_size(axis)
    state = shifted_from(part, axis, 1)
    distance = 1
    while distance < count - 1:
        state = combine(shifted_from(state, axis, distance), state)
        distance *= 2
    return state


def halving_scatter(rows, axis):
    count = lax.axis_size(axis)
    place = lax.axis_index(axis)
    mask = count // 2
    while mask >= 1:
        pairs = rows.reshape((2, rows.shape[0] // 2) + rows.shape[1:])
        upper = (place // mask) % 2 == 1
        keep = jnp.where(upper, pairs[1], pairs[0])
        send = jnp.where(upper, pairs[0], pairs[1])
        route = [(i, i ^ mask) for i in range(count)]
        rows = keep + lax.ppermute(send, axis, route)
        mask //= 2
    return rows[0]


def silu_slope(pre_act):
    sigma = jax.nn.sigmoid(pre_act)
    return sigma * (1.0 + pre_act * (1.0 - sigma))


def later_first(earlier, later):
    decay_high, state_high = earlier
    decay_low, state_low = later
    return (decay_low * decay_high, state_low + decay_low[:, None, None] * state_high)


def block_product(writes, readers, cumulative, upstream):
    scores = lax.dot_general(
        writes, readers, (((0,), (0,)), ((), ())), preferred_element_type=jnp.float32
    )
    span_len = scores.shape[0]
    row_ids = lax.broadcasted_iota(jnp.int32, (span_len, span_len), 0)
    col_ids = lax.broadcasted_iota(jnp.int32, (span_len, span_len), 1)
    causal = col_ids >= row_ids
    head_count = cumulative.shape[1]
    group_size = min(group_heads, head_count)
    pieces = []
    for first_head in range(0, head_count, group_size):
        head_rates = cumulative[:, first_head : first_head + group_size].T
        spread = head_rates[:, None, :] - head_rates[:, :, None]
        weights = jnp.where(
            causal[None], jnp.exp(jnp.minimum(spread, 0.0)) * scores[None], 0.0
        ).astype(jnp.bfloat16)
        pieces.append(
            jnp.einsum(
                "hst,thp->shp",
                weights,
                upstream[:, first_head : first_head + group_size, :],
                preferred_element_type=jnp.float32,
            )
        )
    return jnp.concatenate(pieces, axis=1)


def block_summary(readers, cumulative, upstream):
    weighted = (readers.astype(jnp.float32)[None, :, :] * jnp.exp(cumulative).T[:, None, :]).astype(
        jnp.bfloat16
    )
    return jnp.einsum("hnt,thp->hnp", weighted, upstream, preferred_element_type=jnp.float32)


def conv_grads(grad_pre, padded, weight):
    token_count = grad_pre.shape[0]
    tap_count = weight.shape[0]
    after_rows = from_behind(grad_pre[: tap_count - 1], ("seq", "dp"), -1)
    extended = jnp.concatenate([grad_pre, after_rows], axis=0)
    input_grad = jnp.zeros(grad_pre.shape, jnp.float32)
    weight_terms = []
    for tap_pos in range(tap_count):
        input_grad = (
            input_grad + weight[tap_pos][None, :] * extended[tap_pos : tap_pos + token_count]
        )
        begin = tap_count - 1 - tap_pos
        weight_terms.append(
            jnp.sum(grad_pre * padded[begin : begin + token_count].astype(jnp.float32), axis=0)
        )
    return input_grad, jnp.stack(weight_terms, axis=0), jnp.sum(grad_pre, axis=0)


def layer_body(
    layer_input, conv_weight, conv_bias, log_decay, state_write, state_read, skip_gain, grad_out
):
    inputs = layer_input[0]
    weight = conv_weight[0]
    bias_row = conv_bias[0]
    decay_rates = log_decay[0]
    writes = state_write[0]
    readers = state_read[0]
    skip_row = skip_gain[0]
    upstream = grad_out[0]
    token_count, channels = inputs.shape
    head_count = decay_rates.shape[1]
    head_size = channels // head_count
    state_size = writes.shape[0]
    tap_count = weight.shape[0]
    prior_rows = from_behind(inputs[token_count - (tap_count - 1) :], ("seq", "dp"), 1)
    padded = jnp.concatenate([prior_rows, inputs], axis=0)
    pre_act = jnp.broadcast_to(bias_row[None, :], (token_count, channels))
    for tap_pos in range(tap_count):
        begin = tap_count - 1 - tap_pos
        pre_act = pre_act + weight[tap_pos][None, :] * padded[begin : begin + token_count].astype(
            jnp.float32
        )
    active = jax.nn.silu(pre_act)
    blocks = token_count // STRETCH
    grad_heads = upstream.reshape(token_count, head_count, head_size)
    block_idx = 0
    cumulative = jnp.cumsum(decay_rates, axis=0)
    local_parts = [block_product(writes, readers, cumulative, grad_heads)]
    summaries = [block_summary(readers, cumulative, grad_heads)]
    cumulatives = [cumulative]
    device_decay = jnp.ones((head_count,), jnp.float32)
    device_state = jnp.zeros((head_count, state_size, head_size), jnp.float32)
    for block_idx in reversed(range(blocks)):
        device_decay, device_state = later_first(
            (device_decay, device_state),
            (jnp.exp(cumulatives[block_idx][-1]), summaries[block_idx]),
        )
    carried = carried_in((device_decay, device_state), ("seq", "dp"), later_first)
    carry_state = carried[1]
    cumulative = cumulatives[0]
    block_total = cumulative[-1]
    local_part = local_parts[0]
    skip_term = jnp.sum(
        grad_heads.astype(jnp.float32) * active.reshape(token_count, head_count, head_size),
        axis=(0, 2),
    )
    pieces = 8
    head_span = head_count // pieces
    span = head_span * head_size
    passed_parts, weight_parts, bias_parts = [], [], []
    for piece in range(pieces):
        heads = slice(piece * head_span, (piece + 1) * head_span)
        cols = slice(piece * span, (piece + 1) * span)
        carried_part = jnp.einsum(
            "ns,hnp->shp", writes.astype(jnp.float32), carry_state[heads], precision=HIGH
        )
        carried_part = carried_part * jnp.exp(block_total[None, heads] - cumulative[:, heads])[:, :, None]
        grad_act = (
            local_part[:, heads]
            + carried_part
            + skip_row[None, heads, None] * grad_heads[:, heads].astype(jnp.float32)
        )
        grad_pre = grad_act.reshape(token_count, span) * silu_slope(pre_act[:, cols])
        piece_grad, piece_weight, piece_bias = conv_grads(grad_pre, padded[:, cols], weight[:, cols])
        piece_grad = piece_grad.astype(jnp.bfloat16)
        passed_parts.append(from_behind(piece_grad[None], "section", -1))
        weight_parts.append(piece_weight)
        bias_parts.append(piece_bias)
    weight_grad = jnp.concatenate(weight_parts, axis=1)
    bias_grad = jnp.concatenate(bias_parts, axis=0)
    group = ("seq", "dp")
    parts = lax.axis_size(group)
    width = channels // parts
    packed = jnp.concatenate(
        [
            weight_grad.reshape(tap_count, parts, width).transpose(1, 0, 2).reshape(parts, tap_count * width),
            bias_grad.reshape(parts, width),
            skip_term.reshape(parts, head_count // parts),
        ],
        axis=1,
    )
    owned = halving_scatter(packed, group)
    shares = (
        owned[: tap_count * width].reshape(tap_count, width),
        owned[tap_count * width : (tap_count + 1) * width],
        owned[(tap_count + 1) * width :],
    )
    passed = jnp.concatenate(passed_parts, axis=2)
    return (passed, shares[0][None], shares[1][None], shares[2][None])


def solution(mesh):
    placed = (
        P("section", ("seq", "dp"), None),
        P("section", None, None),
        P("section", None),
        P("section", ("seq", "dp"), None),
        P("section", None, ("seq", "dp")),
        P("section", None, ("seq", "dp")),
        P("section", None),
        P("section", ("seq", "dp"), None),
    )
    return jax.shard_map(
        layer_body,
        mesh=mesh,
        in_specs=placed,
        out_specs=(
            P("section", ("seq", "dp"), None),
            P("section", None, ("seq", "dp")),
            P("section", ("seq", "dp")),
            P("section", ("seq", "dp")),
        ),
        check_vma=False,
    )
```

```python
import jax
import jax.numpy as jnp
from jax import lax
from jax.sharding import PartitionSpec as P

STRETCH = 256


HIGH = lax.Precision.HIGHEST
group_heads = 32


def from_behind(block, axis, distance):
    devices = range(lax.axis_size(axis))
    route = [(i - distance, i) for i in devices if i - distance in devices]
    return lax.ppermute(block, axis, route)


def shifted_from(part, axis, distance):
    count = lax.axis_size(axis)
    route = [(i + distance, i) for i in range(count) if i + distance < count]
    return jax.tree.map(lambda a: lax.ppermute(a, axis, route), part)


def carried_in(part, axis, combine):
    count = lax.axis_size(axis)
    state = shifted_from(part, axis, 1)
    distance = 1
    while distance < count - 1:
        state = combine(shifted_from(state, axis, distance), state)
        distance *= 2
    return state


def halving_scatter(rows, axis):
    count = lax.axis_size(axis)
    place = lax.axis_index(axis)
    mask = 1
    while mask < count:
        pairs = rows.reshape((rows.shape[0] // 2, 2) + rows.shape[1:])
        upper = (place // mask) % 2 == 1
        keep = jnp.where(upper, pairs[:, 1], pairs[:, 0])
        send = jnp.where(upper, pairs[:, 0], pairs[:, 1])
        route = [(i, i ^ mask) for i in range(count)]
        rows = keep + lax.ppermute(send, axis, route)
        mask *= 2
    return rows[0]


def silu_slope(pre_act):
    sigma = jax.nn.sigmoid(pre_act)
    return sigma * (1.0 + pre_act * (1.0 - sigma))


def later_first(earlier, later):
    decay_high, state_high = earlier
    decay_low, state_low = later
    return (decay_low * decay_high, state_low + decay_low[:, None, None] * state_high)


def block_product(writes, readers, cumulative, upstream):
    scores = lax.dot_general(
        writes, readers, (((0,), (0,)), ((), ())), preferred_element_type=jnp.float32
    )
    span_len = scores.shape[0]
    row_ids = lax.broadcasted_iota(jnp.int32, (span_len, span_len), 0)
    col_ids = lax.broadcasted_iota(jnp.int32, (span_len, span_len), 1)
    causal = col_ids >= row_ids
    head_count = cumulative.shape[1]
    group_size = min(group_heads, head_count)
    pieces = []
    for first_head in range(0, head_count, group_size):
        head_rates = cumulative[:, first_head : first_head + group_size].T
        spread = head_rates[:, None, :] - head_rates[:, :, None]
        weights = jnp.where(
            causal[None], jnp.exp(jnp.minimum(spread, 0.0)) * scores[None], 0.0
        ).astype(jnp.bfloat16)
        pieces.append(
            jnp.einsum(
                "hst,thp->shp",
                weights,
                upstream[:, first_head : first_head + group_size, :],
                preferred_element_type=jnp.float32,
            )
        )
    return jnp.concatenate(pieces, axis=1)


def block_summary(readers, cumulative, upstream):
    weighted = (readers.astype(jnp.float32)[None, :, :] * jnp.exp(cumulative).T[:, None, :]).astype(
        jnp.bfloat16
    )
    return jnp.einsum("hnt,thp->hnp", weighted, upstream, preferred_element_type=jnp.float32)


def conv_grads(grad_pre, padded, weight):
    token_count = grad_pre.shape[0]
    tap_count = weight.shape[0]
    after_rows = from_behind(grad_pre[: tap_count - 1], ("seq", "dp"), -1)
    extended = jnp.concatenate([grad_pre, after_rows], axis=0)
    input_grad = jnp.zeros(grad_pre.shape, jnp.float32)
    weight_terms = []
    for tap_pos in range(tap_count):
        input_grad = (
            input_grad + weight[tap_pos][None, :] * extended[tap_pos : tap_pos + token_count]
        )
        begin = tap_count - 1 - tap_pos
        weight_terms.append(
            jnp.sum(grad_pre * padded[begin : begin + token_count].astype(jnp.float32), axis=0)
        )
    return input_grad, jnp.stack(weight_terms, axis=0), jnp.sum(grad_pre, axis=0)


def layer_body(
    layer_input, conv_weight, conv_bias, log_decay, state_write, state_read, skip_gain, grad_out
):
    inputs = layer_input[0]
    weight = conv_weight[0]
    bias_row = conv_bias[0]
    decay_rates = log_decay[0]
    writes = state_write[0]
    readers = state_read[0]
    skip_row = skip_gain[0]
    upstream = grad_out[0]
    token_count, channels = inputs.shape
    head_count = decay_rates.shape[1]
    head_size = channels // head_count
    state_size = writes.shape[0]
    tap_count = weight.shape[0]
    prior_rows = from_behind(inputs[token_count - (tap_count - 1) :], ("seq", "dp"), 1)
    padded = jnp.concatenate([prior_rows, inputs], axis=0)
    pre_act = jnp.broadcast_to(bias_row[None, :], (token_count, channels))
    for tap_pos in range(tap_count):
        begin = tap_count - 1 - tap_pos
        pre_act = pre_act + weight[tap_pos][None, :] * padded[begin : begin + token_count].astype(
            jnp.float32
        )
    active = jax.nn.silu(pre_act)
    blocks = token_count // STRETCH
    grad_heads = upstream.reshape(token_count, head_count, head_size)
    block_idx = 0
    cumulative = jnp.cumsum(decay_rates, axis=0)
    local_parts = [block_product(writes, readers, cumulative, grad_heads)]
    summaries = [block_summary(readers, cumulative, grad_heads)]
    cumulatives = [cumulative]
    device_decay = jnp.ones((head_count,), jnp.float32)
    device_state = jnp.zeros((head_count, state_size, head_size), jnp.float32)
    for block_idx in reversed(range(blocks)):
        device_decay, device_state = later_first(
            (device_decay, device_state),
            (jnp.exp(cumulatives[block_idx][-1]), summaries[block_idx]),
        )
    carried = carried_in((device_decay, device_state), ("seq", "dp"), later_first)
    carry_state = carried[1]
    cumulative = cumulatives[0]
    block_total = cumulative[-1]
    local_part = local_parts[0]
    skip_term = jnp.sum(
        grad_heads.astype(jnp.float32) * active.reshape(token_count, head_count, head_size),
        axis=(0, 2),
    )
    pieces = 4
    head_span = head_count // pieces
    span = head_span * head_size
    passed_parts, weight_parts, bias_parts = [], [], []
    for piece in range(pieces):
        heads = slice(piece * head_span, (piece + 1) * head_span)
        cols = slice(piece * span, (piece + 1) * span)
        carried_part = jnp.einsum(
            "ns,hnp->shp", writes.astype(jnp.float32), carry_state[heads], precision=HIGH
        )
        carried_part = carried_part * jnp.exp(block_total[None, heads] - cumulative[:, heads])[:, :, None]
        grad_act = (
            local_part[:, heads]
            + carried_part
            + skip_row[None, heads, None] * grad_heads[:, heads].astype(jnp.float32)
        )
        grad_pre = grad_act.reshape(token_count, span) * silu_slope(pre_act[:, cols])
        piece_grad, piece_weight, piece_bias = conv_grads(grad_pre, padded[:, cols], weight[:, cols])
        piece_grad = piece_grad.astype(jnp.bfloat16)
        passed_parts.append(from_behind(piece_grad[None], "section", -1))
        weight_parts.append(piece_weight)
        bias_parts.append(piece_bias)
    weight_grad = jnp.concatenate(weight_parts, axis=1)
    bias_grad = jnp.concatenate(bias_parts, axis=0)
    group = ("seq", "dp")
    parts = lax.axis_size(group)
    width = channels // parts
    packed = jnp.concatenate(
        [
            weight_grad.reshape(tap_count, parts, width).transpose(1, 0, 2).reshape(parts, tap_count * width),
            bias_grad.reshape(parts, width),
            skip_term.reshape(parts, head_count // parts),
        ],
        axis=1,
    )
    owned = halving_scatter(packed, group)
    shares = (
        owned[: tap_count * width].reshape(tap_count, width),
        owned[tap_count * width : (tap_count + 1) * width],
        owned[(tap_count + 1) * width :],
    )
    passed = jnp.concatenate(passed_parts, axis=2)
    return (passed, shares[0][None], shares[1][None], shares[2][None])


def solution(mesh):
    placed = (
        P("section", ("seq", "dp"), None),
        P("section", None, None),
        P("section", None),
        P("section", ("seq", "dp"), None),
        P("section", None, ("seq", "dp")),
        P("section", None, ("seq", "dp")),
        P("section", None),
        P("section", ("seq", "dp"), None),
    )
    return jax.shard_map(
        layer_body,
        mesh=mesh,
        in_specs=placed,
        out_specs=(
            P("section", ("seq", "dp"), None),
            P("section", None, ("seq", "dp")),
            P("section", ("seq", "dp")),
            P("section", ("seq", "dp")),
        ),
        check_vma=False,
    )
```
